32 devices in a mesh: grp: 2 (over x), node: 16 (over z, y, core).
Axes of the slice: x: 2, y: 2, z: 4, core: 2. Of those that a mesh axis runs over, the one named last changes fastest.
Arguments:
- nodes: bfloat16 [128, 2, 1024, 1024], P('grp', None, 'node'), parts along dimension 0, may hold values from -0.34960938 to 0.34960938
- pair_nodes: int32 [16, 2], replicated, may hold values from 0 to 63
- prod_left: int32 [16], replicated, may hold values from 0 to 15, as said below
- prod_right: int32 [16], replicated, may hold values from 0 to 15, each once
- prod_flag: int32 [16], replicated, may hold values from 0 to 1
- prod_diag: int32 [16], replicated, may hold values from 0 to 7, as said below
Outputs:
- diagrams: bfloat16 [16, 2, 1024, 1024], P('grp', None, 'node'), parts along dimension 0
The draws below stay inside these ranges and needn't reach their ends.
There are 2 independent parts, one for each index of `grp`. The reference program is written for one: setup_inputs(seed, part) draws one part's arguments, and reference() takes and returns one part's arrays. A program takes and returns all parts, laid end to end along the dimension named above; an argument that names none is the same for every part. Nothing has to cross between parts.
Inputs may be any that keep to these rules, and one draw needn't show every extreme that they name: `prod_left`: exactly 8 distinct pairs are left operands, each of exactly two products. `prod_diag`: every diagram receives exactly two products.
All inputs are finite; a program needn't handle non-finite values.
Results may differ from the reference program's by a relative error of at most 0.0065.
Values may be sent and summed in bfloat16 or wider, within the bound.
A program may use at most 128 MiB of HBM per device.

```python
import jax
import jax.numpy as jnp
from jax import lax

M = 1024
NODES = 64
PAIRS = 16
PRODS = 16
DIAGS = 8


def draw_prod_left(key, part):
    base = jax.random.permutation(jax.random.fold_in(key, 11), PAIRS).astype(jnp.int32)
    return base[jnp.arange(PRODS, dtype=jnp.int32) // 2].astype(jnp.int32)


def draw_prod_diag(key, part):
    order = jax.random.permutation(jax.random.fold_in(key, 23), PRODS).astype(jnp.int32)
    return (order % DIAGS).astype(jnp.int32)


def plant(result, key, low, top_value):
    longest = result.shape.index(max(result.shape))
    spots = []
    for shift in (0, 1):
        where = [jax.random.randint(jax.random.fold_in(key, axis), (), 0, length) for axis, length in enumerate(result.shape)]
        where[longest] = (where[longest] + shift) % result.shape[longest]
        spots.append(tuple(where))
    return result.at[spots[0]].set(low).at[spots[1]].set(top_value)


def steps_of(stream_key, shape, shards, low, top_value):
    gain = 1.0
    for position, blocks in shards:
        draws = jax.random.uniform(jax.random.fold_in(jax.random.fold_in(stream_key, 6), position), (blocks,), jnp.float32, low / len(shards), top_value / len(shards))
        gain = gain * jnp.repeat(jnp.exp(draws), shape[position] // blocks).reshape((-1,) + (1,) * (len(shape) - 1 - position))
    return gain


def noise(own_key, shape, spread, bound, pieces=(), held_as=jnp.bfloat16):
    array = spread * jax.random.normal(own_key, shape, jnp.float32)
    if pieces:
        array = array * steps_of(own_key, shape, pieces, -0.22, 0.18)
    return jnp.clip(array, -bound, bound).astype(held_as)


def setup_inputs(seed: int = 0, part: int = 0) -> dict:
    keys = jax.random.split(jax.random.key(seed), 7)
    own_keys = jax.random.split(jax.random.fold_in(keys[6], part), 7)
    return {
        "nodes": noise(own_keys[0], (NODES, 2, M, M), 0.0573, 0.34960938, ((2, 16),)),
        "pair_nodes": plant(jax.random.randint(keys[1], (PAIRS, 2), 0, NODES), jax.random.fold_in(keys[1], 1), 0, NODES - 1).astype(jnp.int32),
        "prod_left": draw_prod_left(jax.random.fold_in(keys[6], 71), part),
        "prod_right": jax.random.permutation(keys[3], PAIRS).astype(jnp.int32),
        "prod_flag": plant(jax.random.randint(keys[4], (PRODS,), 0, 2), jax.random.fold_in(keys[4], 1), 0, 1).astype(jnp.int32),
        "prod_diag": draw_prod_diag(jax.random.fold_in(keys[6], 71), part),
    }


def complex_product(left_re, left_im, right_re, right_im):
    real_part = jnp.dot(left_re, right_re, preferred_element_type=jnp.float32) - jnp.dot(left_im, right_im, preferred_element_type=jnp.float32)
    imag_part = jnp.dot(left_re, right_im, preferred_element_type=jnp.float32) + jnp.dot(left_im, right_re, preferred_element_type=jnp.float32)
    return jnp.stack([real_part, imag_part]).astype(jnp.bfloat16)


def reference(nodes, pair_nodes, prod_left, prod_right, prod_flag, prod_diag):
    def pair_one(entry):
        left_node = nodes[entry[0]]
        right_node = nodes[entry[1]]
        return complex_product(left_node[0], left_node[1], right_node[0], right_node[1])

    paired = lax.map(pair_one, pair_nodes)

    def second_one(entry):
        left_pair = paired[entry[0]]
        right_pair = paired[entry[1]]
        flipped = entry[2] == 1
        left_re = jnp.where(flipped, left_pair[0].T, left_pair[0])
        left_im = jnp.where(flipped, -left_pair[1].T, left_pair[1])
        return complex_product(left_re, left_im, right_pair[0], right_pair[1])

    entries = jnp.stack([prod_left, prod_right, prod_flag], axis=1)
    results = lax.map(second_one, entries)
    diagram_map = (prod_diag[None, :] == jnp.arange(DIAGS, dtype=jnp.int32)[:, None]).astype(jnp.float32)
    summed = jnp.dot(diagram_map, results.reshape(PRODS, -1).astype(jnp.float32), precision=lax.Precision.HIGHEST)
    return summed.reshape(DIAGS, 2, M, M).astype(jnp.bfloat16)
```

```python
import functools

import jax
import jax.numpy as jnp
from jax import lax
from jax.experimental import pallas as pl
from jax.experimental.pallas import tpu as pltpu
from jax.sharding import PartitionSpec as P

TILE = 256


def gather_kernel(left_ids, a_ids, b_ids, left_in, a_in, b_in, left_out, a_out, b_out):
    del left_ids, a_ids, b_ids
    left_out[...] = left_in[...]
    a_out[...] = a_in[...]
    chunks = b_out.shape[0]
    width = b_out.shape[-1]
    for c in range(chunks):
        b_out[c] = b_in[:, :, :, c * width : (c + 1) * width]


def gather(nodes, left_ids, a_ids, b_ids, chunks):
    count = a_ids.shape[0]
    _, parts, rows, order = nodes.shape
    width = order // chunks
    block = (1, parts, rows, order)
    whole = jax.ShapeDtypeStruct((count, parts, rows, order), nodes.dtype)
    cut = jax.ShapeDtypeStruct((chunks, count, parts, rows, width), nodes.dtype)
    return pl.pallas_call(
        gather_kernel,
        out_shape=(whole, whole, cut),
        grid_spec=pltpu.PrefetchScalarGridSpec(
            num_scalar_prefetch=3,
            grid=(count,),
            in_specs=[
                pl.BlockSpec(block, lambda i, l, a, b: (l[i], 0, 0, 0)),
                pl.BlockSpec(block, lambda i, l, a, b: (a[i], 0, 0, 0)),
                pl.BlockSpec(block, lambda i, l, a, b: (b[i], 0, 0, 0)),
            ],
            out_specs=[
                pl.BlockSpec(block, lambda i, l, a, b: (i, 0, 0, 0)),
                pl.BlockSpec(block, lambda i, l, a, b: (i, 0, 0, 0)),
                pl.BlockSpec((chunks, 1, parts, rows, width), lambda i, l, a, b: (0, i, 0, 0, 0)),
            ],
        ),
        compiler_params=pltpu.CompilerParams(vmem_limit_bytes=16 * 2**20),
    )(left_ids, a_ids, b_ids, nodes, nodes, nodes)


def tile_product(left_re, left_im, right_re, right_im):
    dot = functools.partial(jnp.dot, preferred_element_type=jnp.float32)
    real_part = dot(left_re, right_re) - dot(left_im, right_im)
    imag_part = dot(left_re, right_im) + dot(left_im, right_re)
    return real_part.astype(jnp.bfloat16), imag_part.astype(jnp.bfloat16)


def exchange_kernel(
    n,
    flags,
    slots,
    left_send,
    a_send,
    b_send,
    out,
    lefts,
    a_full,
    b_full,
    left_plain,
    left_used,
    right_pair,
    result,
    panels,
    left_sem,
    a_sem,
    b_sem,
    swap_sem,
    result_sem,
    left_out_sem,
    a_out_sem,
    b_out_sem,
    swap_out_sem,
    result_out_sem,
):
    me = lax.axis_index("node")
    parity = lax.rem(me, 2)
    partner = me + 1 - 2 * parity
    chunks = b_full.shape[0]
    order = a_full.shape[1]
    rows = left_send.shape[2]
    tiles = order // TILE
    my_rows = pl.ds(pl.multiple_of(me * rows, rows), rows)

    def target(t):
        half = lax.div(t + 1, 2)
        return lax.rem(me + n // 2 + (2 * lax.rem(t, 2) - 1) * half, n)

    barrier = pltpu.get_barrier_semaphore()

    @pl.loop(0, n - 1)
    def _(t):
        pl.semaphore_signal(
            barrier,
            inc=1,
            device_id={"node": target(t)},
            device_id_type=pl.DeviceIdType.MESH,
        )

    pl.semaphore_wait(barrier, n - 1)

    def push(src, dst, send_sem, recv_sem, to):
        pltpu.make_async_remote_copy(
            src_ref=src,
            dst_ref=dst,
            send_sem=send_sem,
            recv_sem=recv_sem,
            device_id={"node": to},
            device_id_type=pl.DeviceIdType.MESH,
        ).start()

    def landed(ref, sem):
        pltpu.make_async_copy(ref, ref, sem).wait()

    @pl.loop(0, n - 1)
    def _(t):
        to = target(t)
        push(left_send.at[to], lefts.at[lax.rem(to, 2), :, my_rows], left_out_sem, left_sem, to)

    pltpu.make_async_copy(left_send.at[me], lefts.at[parity, :, my_rows], left_sem).start()

    @pl.loop(0, n - 1)
    def _(t):
        to = target(t)
        push(a_send.at[to], a_full.at[:, my_rows], a_out_sem, a_sem, to)

    pltpu.make_async_copy(a_send.at[me], a_full.at[:, my_rows], a_sem).start()

    @pl.loop(0, chunks)
    def _(c):
        @pl.loop(0, n - 1)
        def _(t):
            to = target(t)
            push(b_send.at[c, to], b_full.at[c, :, my_rows], b_out_sem.at[c], b_sem.at[c], to)

        pltpu.make_async_copy(b_send.at[c, me], b_full.at[c, :, my_rows], b_sem.at[c]).start()

    landed(lefts.at[parity], left_sem)
    push(lefts.at[parity], lefts.at[parity], swap_out_sem, swap_sem, partner)
    landed(lefts.at[1 - parity], swap_sem)

    def block(i):
        return pl.ds(pl.multiple_of(i * TILE, TILE), TILE)

    @pl.loop(0, tiles * tiles)
    def _(t):
        down, across = block(lax.div(t, tiles)), block(lax.rem(t, tiles))
        real_part, imag_part = tile_product(
            lefts[0, 0, down, :], lefts[0, 1, down, :], lefts[1, 0, :, across], lefts[1, 1, :, across]
        )
        left_plain[0, down, across] = real_part
        left_plain[1, down, across] = imag_part

    flipped = flags[me] == 1

    @pl.loop(0, tiles * tiles)
    def _(t):
        down, across = block(lax.div(t, tiles)), block(lax.rem(t, tiles))
        left_used[0, down, across] = jnp.where(
            flipped, left_plain[0, across, down].T, left_plain[0, down, across]
        )
        left_used[1, down, across] = jnp.where(
            flipped, -left_plain[1, across, down].T, left_plain[1, down, across]
        )

    landed(a_full, a_sem)

    for c in range(chunks):
        landed(b_full.at[c], b_sem.at[c])

        @pl.loop(0, tiles)
        def _(i):
            down = block(i)
            real_part, imag_part = tile_product(
                a_full[0, down, :], a_full[1, down, :], b_full[c, 0], b_full[c, 1]
            )
            right_pair[0, down, :] = real_part
            right_pair[1, down, :] = imag_part

        @pl.loop(0, tiles)
        def _(i):
            down = block(i)
            real_part, imag_part = tile_product(
                left_used[0, down, :], left_used[1, down, :], right_pair[0], right_pair[1]
            )
            result[c, 0, down, :] = real_part
            result[c, 1, down, :] = imag_part

        @pl.loop(0, n - 1)
        def _(t):
            to = target(t)
            to_rows = pl.ds(pl.multiple_of(to * rows, rows), rows)
            push(
                result.at[c, :, to_rows],
                panels[c].at[me],
                result_out_sem.at[c],
                result_sem.at[c],
                to,
            )

        pltpu.make_async_copy(
            result.at[c, :, my_rows], panels[c].at[me], result_sem.at[c]
        ).start()

    width = b_full.shape[-1]
    for c in range(chunks):
        landed(panels[c], result_sem.at[c])

        @pl.loop(0, out.shape[0])
        def _(d):
            first = panels[c][slots[d, 0]].astype(jnp.float32)
            second = panels[c][slots[d, 1]].astype(jnp.float32)
            out[d, :, :, c * width : (c + 1) * width] = (first + second).astype(out.dtype)

    others = pl.ds(0, n - 1)
    landed(left_send.at[others], left_out_sem)
    landed(a_send.at[others], a_out_sem)
    landed(lefts.at[parity], swap_out_sem)
    for c in range(chunks):
        landed(b_send.at[c, others], b_out_sem.at[c])
        landed(panels[c].at[others], result_out_sem.at[c])


def local(nodes, pair_nodes, prod_left, prod_right, prod_flag, prod_diag, *, n):
    _, parts, rows, order = nodes.shape
    count = prod_left.shape[0]
    assert count == n and rows * n == order
    diags = count // 2
    chunks = order // TILE
    numbers = jnp.arange(count, dtype=jnp.int32)
    ahead = (prod_left[None, :] < prod_left[:, None]) | (
        (prod_left[None, :] == prod_left[:, None]) & (numbers[None, :] < numbers[:, None])
    )
    rank = jnp.sum(ahead.astype(jnp.int32), axis=1)
    here = rank[None, :] == numbers[:, None]

    def ordered(values):
        return jnp.sum(jnp.where(here, values[None, :], 0), axis=1)

    left_of, right_of = ordered(prod_left), ordered(prod_right)
    flag_of, diag_of = ordered(prod_flag), ordered(prod_diag)

    def node_of(pairs, side):
        hot = pairs[:, None] == jnp.arange(pair_nodes.shape[0], dtype=jnp.int32)[None, :]
        return jnp.sum(jnp.where(hot, side, 0), axis=1)

    side = jnp.where(numbers[:, None] % 2 == 0, pair_nodes[None, :, 0], pair_nodes[None, :, 1])
    left_ids = node_of(left_of, side)
    a_ids = node_of(right_of, pair_nodes[None, :, 0])
    b_ids = node_of(right_of, pair_nodes[None, :, 1])
    mine = diag_of[None, :] == jnp.arange(diags, dtype=jnp.int32)[:, None]
    first = jnp.min(jnp.where(mine, numbers[None, :], count), axis=1)
    last = jnp.max(jnp.where(mine, numbers[None, :], -1), axis=1)
    slots = jnp.stack([first, last], axis=1)

    left_send, a_send, b_send = gather(nodes, left_ids, a_ids, b_ids, chunks)
    width = order // chunks
    kind = nodes.dtype
    dma = pltpu.SemaphoreType.DMA
    smem = pl.BlockSpec(memory_space=pltpu.SMEM)
    anywhere = pl.BlockSpec(memory_space=pl.ANY)
    return pl.pallas_call(
        functools.partial(exchange_kernel, n),
        out_shape=jax.ShapeDtypeStruct((diags, parts, rows, order), kind),
        in_specs=[smem, smem, anywhere, anywhere, anywhere],
        out_specs=pl.BlockSpec(memory_space=pltpu.VMEM),
        scratch_shapes=[
            pltpu.VMEM((2, parts, order, order), kind),
            pltpu.VMEM((parts, order, order), kind),
            pltpu.VMEM((chunks, parts, order, width), kind),
            pltpu.VMEM((parts, order, order), kind),
            pltpu.VMEM((parts, order, order), kind),
            pltpu.VMEM((parts, order, width), kind),
            pltpu.VMEM((chunks, parts, order, width), kind),
            [pltpu.VMEM((count, parts, rows, width), kind)] * chunks,
            dma,
            dma,
            dma((chunks,)),
            dma,
            dma((chunks,)),
            dma,
            dma,
            dma((chunks,)),
            dma,
            dma((chunks,)),
        ],
        compiler_params=pltpu.CompilerParams(
            collective_id=0, has_side_effects=True, vmem_limit_bytes=56 * 2**20
        ),
    )(flag_of, slots, left_send, a_send, b_send)


def solution(mesh):
    placed = (P("grp", None, "node", None), P(), P(), P(), P(), P())
    return jax.shard_map(
        functools.partial(local, n=mesh.shape["node"]),
        mesh=mesh,
        in_specs=placed,
        out_specs=P("grp", None, "node", None),
        check_vma=False,
    )
```

```python
import functools

import jax
import jax.numpy as jnp
from jax import lax
from jax.experimental import pallas as pl
from jax.experimental.pallas import tpu as pltpu
from jax.sharding import PartitionSpec as P

TILE = 256


def plan_and_gather_kernel(
    pair_nodes,
    prod_left,
    prod_right,
    prod_flag,
    prod_diag,
    nodes,
    flags,
    merges,
    finals,
    left_out,
    a_out,
    b_out,
    seen_left,
    seen_diag,
    mate_left,
    mate_diag,
    done,
    slot_of,
    order,
    left_sem,
    a_sem,
    b_sem,
):
    count = prod_left.shape[0]
    diags = count // 2
    half = count // 2
    slots = half // 2 + 1
    chunks = b_out.shape[0]
    width = b_out.shape[-1]

    @pl.loop(0, pair_nodes.shape[0])
    def _(p):
        seen_left[p] = -1

    @pl.loop(0, diags)
    def _(d):
        seen_diag[d] = -1
        slot_of[d] = -1
        slot_of[diags + d] = -1

    @pl.loop(0, count)
    def _(k):
        done[k] = 0
        for group, seen, mate in (
            (prod_left[k], seen_left, mate_left),
            (prod_diag[k], seen_diag, mate_diag),
        ):
            earlier = seen[group]
            found = earlier >= 0
            mate[k] = earlier
            back = jnp.where(found, earlier, k)
            mate[back] = jnp.where(found, k, mate[back])
            seen[group] = k

    def place(g, now):
        other = mate_left[now]
        done[now] = 1
        done[other] = 1
        order[2 * g] = now
        order[2 * g + 1] = other
        for at, k in ((2 * g, now), (2 * g + 1, other)):
            flags[at] = prod_flag[k]
            left_id = pair_nodes[prod_left[k], at - 2 * g]
            right = prod_right[k]
            pltpu.make_async_copy(nodes.at[left_id], left_out.at[at], left_sem).start()
            pltpu.make_async_copy(nodes.at[pair_nodes[right, 0]], a_out.at[at], a_sem).start()
            for c in range(chunks):
                pltpu.make_async_copy(
                    nodes.at[pair_nodes[right, 1], :, :, pl.ds(c * width, width)],
                    b_out.at[c, at],
                    b_sem,
                ).start()
        free = lax.fori_loop(
            0,
            count,
            lambda k, best: jnp.where(done[count - 1 - k] == 0, count - 1 - k, best),
            jnp.int32(0),
        )
        follow = mate_diag[other]
        return jnp.where(done[follow] == 0, follow, free)

    lax.fori_loop(0, count // 2, place, jnp.int32(0))

    for h in range(2):
        base = h * slots

        @pl.loop(0, slots)
        def _(t):
            merges[2 * (base + t)] = half
            merges[2 * (base + t) + 1] = half

        def take(i, used):
            diag = prod_diag[order[h * half + i]]
            slot = slot_of[h * diags + diag]
            new = slot < 0
            slot = jnp.where(new, used, slot)
            slot_of[h * diags + diag] = slot
            at = 2 * (base + slot)
            merges[at] = jnp.where(new, i, merges[at])
            merges[at + 1] = jnp.where(new, half, i)
            return used + new.astype(jnp.int32)

        lax.fori_loop(0, half, take, jnp.int32(0))

    for h in range(2):

        @pl.loop(0, diags)
        def _(d):
            near = slot_of[h * diags + d]
            far = half + slot_of[(1 - h) * diags + d]
            here = near >= 0
            at = 2 * (h * slots + jnp.maximum(near, 0))
            both = here & (merges[at + 1] < half)
            finals[2 * (h * diags + d)] = jnp.where(here, merges[at], far)
            finals[2 * (h * diags + d) + 1] = jnp.where(
                both, merges[at + 1], jnp.where(here, far, half + slots)
            )

    pltpu.make_async_copy(left_out, left_out, left_sem).wait()
    pltpu.make_async_copy(a_out, a_out, a_sem).wait()
    pltpu.make_async_copy(b_out, b_out, b_sem).wait()


def plan_and_gather(nodes, pair_nodes, prod_left, prod_right, prod_flag, prod_diag, chunks):
    count = prod_left.shape[0]
    _, parts, rows, order = nodes.shape
    half = count // 2
    slots = half // 2 + 1
    whole = jax.ShapeDtypeStruct((count, parts, rows, order), nodes.dtype)
    cut = jax.ShapeDtypeStruct((chunks, count, parts, rows, order // chunks), nodes.dtype)
    table = lambda size: jax.ShapeDtypeStruct((size,), jnp.int32)
    smem = pl.BlockSpec(memory_space=pltpu.SMEM)
    anywhere = pl.BlockSpec(memory_space=pl.ANY)
    scratch = lambda size: pltpu.SMEM((size,), jnp.int32)
    return pl.pallas_call(
        plan_and_gather_kernel,
        out_shape=(table(count), table(4 * slots), table(4 * half), whole, whole, cut),
        in_specs=[smem] * 5 + [pl.BlockSpec(memory_space=pltpu.HBM)],
        out_specs=[smem] * 3 + [anywhere] * 3,
        scratch_shapes=[
            scratch(pair_nodes.shape[0]),
            scratch(half),
            scratch(count),
            scratch(count),
            scratch(count),
            scratch(2 * half),
            scratch(count),
            pltpu.SemaphoreType.DMA,
            pltpu.SemaphoreType.DMA,
            pltpu.SemaphoreType.DMA,
        ],
        compiler_params=pltpu.CompilerParams(vmem_limit_bytes=48 * 2**20),
    )(pair_nodes, prod_left, prod_right, prod_flag, prod_diag, nodes)


def tile_product(left_re, left_im, right_re, right_im):
    dot = functools.partial(jnp.dot, preferred_element_type=jnp.float32)
    real_part = dot(left_re, right_re) - dot(left_im, right_im)
    imag_part = dot(left_re, right_im) + dot(left_im, right_re)
    return real_part.astype(jnp.bfloat16), imag_part.astype(jnp.bfloat16)


def exchange_kernel(
    n,
    flags,
    merges,
    finals,
    left_send,
    a_send,
    b_send,
    out,
    lefts,
    a_full,
    b_full,
    left_plain,
    left_used,
    right_pair,
    result,
    panels,
    relayed,
    merged,
    left_sem,
    a_sem,
    b_sem,
    swap_sem,
    result_sem,
    relay_sem,
    far_sem,
    left_out_sem,
    a_out_sem,
    b_out_sem,
    swap_out_sem,
    result_out_sem,
    relay_out_sem,
    far_out_sem,
):
    me = lax.axis_index("node")
    parity = lax.rem(me, 2)
    partner = me + 1 - 2 * parity
    chunks = b_full.shape[0]
    order = a_full.shape[1]
    rows = left_send.shape[2]
    tiles = order // TILE
    my_rows = pl.ds(pl.multiple_of(me * rows, rows), rows)

    def target(t):
        half = lax.div(t + 1, 2)
        return lax.rem(me + n // 2 + (2 * lax.rem(t, 2) - 1) * half, n)

    barrier = pltpu.get_barrier_semaphore()

    @pl.loop(0, n - 1)
    def _(t):
        pl.semaphore_signal(
            barrier,
            inc=1,
            device_id={"node": target(t)},
            device_id_type=pl.DeviceIdType.MESH,
        )

    pl.semaphore_wait(barrier, n - 1)

    def push(src, dst, send_sem, recv_sem, to):
        pltpu.make_async_remote_copy(
            src_ref=src,
            dst_ref=dst,
            send_sem=send_sem,
            recv_sem=recv_sem,
            device_id={"node": to},
            device_id_type=pl.DeviceIdType.MESH,
        ).start()

    def landed(ref, sem):
        pltpu.make_async_copy(ref, ref, sem).wait()

    @pl.loop(0, n - 1)
    def _(t):
        to = target(t)
        push(left_send.at[to], lefts.at[lax.rem(to, 2), :, my_rows], left_out_sem, left_sem, to)

    pltpu.make_async_copy(left_send.at[me], lefts.at[parity, :, my_rows], left_sem).start()

    @pl.loop(0, n - 1)
    def _(t):
        to = target(t)
        push(a_send.at[to], a_full.at[:, my_rows], a_out_sem, a_sem, to)

    pltpu.make_async_copy(a_send.at[me], a_full.at[:, my_rows], a_sem).start()

    @pl.loop(0, chunks)
    def _(c):
        @pl.loop(0, n - 1)
        def _(t):
            to = target(t)
            push(b_send.at[c, to], b_full.at[c, :, my_rows], b_out_sem.at[c], b_sem.at[c], to)

        pltpu.make_async_copy(b_send.at[c, me], b_full.at[c, :, my_rows], b_sem.at[c]).start()

    landed(lefts.at[parity], left_sem)
    push(lefts.at[parity], lefts.at[parity], swap_out_sem, swap_sem, partner)
    landed(lefts.at[1 - parity], swap_sem)

    def block(i):
        return pl.ds(pl.multiple_of(i * TILE, TILE), TILE)

    @pl.loop(0, tiles * tiles)
    def _(t):
        down, across = block(lax.div(t, tiles)), block(lax.rem(t, tiles))
        real_part, imag_part = tile_product(
            lefts[0, 0, down, :], lefts[0, 1, down, :], lefts[1, 0, :, across], lefts[1, 1, :, across]
        )
        left_plain[0, down, across] = real_part
        left_plain[1, down, across] = imag_part

    half = n // 2
    slots = merged.shape[1]
    near, far = pl.ds(0, half), pl.ds(half, slots)
    side, place = lax.div(me, half), lax.rem(me, half)
    mirror = lax.rem(me + half, n)

    def rows_of(device):
        return pl.ds(pl.multiple_of(device * rows, rows), rows)

    for c in range(chunks):
        panels[c][half + slots] = jnp.zeros(panels[c].shape[1:], panels[c].dtype)
        relayed[c][half] = jnp.zeros(relayed[c].shape[1:], relayed[c].dtype)

    flipped = flags[me] == 1

    @pl.loop(0, tiles * tiles)
    def _(t):
        down, across = block(lax.div(t, tiles)), block(lax.rem(t, tiles))
        left_used[0, down, across] = jnp.where(
            flipped, left_plain[0, across, down].T, left_plain[0, down, across]
        )
        left_used[1, down, across] = jnp.where(
            flipped, -left_plain[1, across, down].T, left_plain[1, down, across]
        )

    landed(a_full, a_sem)

    def compute(c):
        landed(b_full.at[c], b_sem.at[c])

        @pl.loop(0, tiles)
        def _(i):
            down = block(i)
            real_part, imag_part = tile_product(
                a_full[0, down, :], a_full[1, down, :], b_full[c, 0], b_full[c, 1]
            )
            right_pair[0, down, :] = real_part
            right_pair[1, down, :] = imag_part

        @pl.loop(0, tiles)
        def _(i):
            down = block(i)
            real_part, imag_part = tile_product(
                left_used[0, down, :], left_used[1, down, :], right_pair[0], right_pair[1]
            )
            result[c, 0, down, :] = real_part
            result[c, 1, down, :] = imag_part

        @pl.loop(1, half)
        def _(t):
            to = side * half + lax.rem(place + t, half)
            push(
                result.at[c, :, rows_of(lax.rem(to + half, n))],
                relayed[c].at[place],
                relay_out_sem.at[c],
                relay_sem.at[c],
                to,
            )

        pltpu.make_async_copy(
            result.at[c, :, rows_of(mirror)], relayed[c].at[place], relay_sem.at[c]
        ).start()

        @pl.loop(1, half)
        def _(t):
            to = side * half + lax.rem(place + t, half)
            push(
                result.at[c, :, rows_of(to)],
                panels[c].at[place],
                result_out_sem.at[c],
                result_sem.at[c],
                to,
            )

        pltpu.make_async_copy(
            result.at[c, :, my_rows], panels[c].at[place], result_sem.at[c]
        ).start()

    def merge(c):
        landed(relayed[c].at[near], relay_sem.at[c])

        @pl.loop(0, slots)
        def _(t):
            at = 2 * (side * slots + t)
            first = relayed[c][merges[at]].astype(jnp.float32)
            second = relayed[c][merges[at + 1]].astype(jnp.float32)
            merged[c, t] = (first + second).astype(merged.dtype)

        push(merged.at[c], panels[c].at[far], far_out_sem.at[c], far_sem.at[c], mirror)

    for c in range(chunks):
        compute(c)
        if c > 0:
            merge(c - 1)
    merge(chunks - 1)

    width = b_full.shape[-1]
    for c in range(chunks):
        landed(panels[c].at[near], result_sem.at[c])
        landed(panels[c].at[far], far_sem.at[c])

        @pl.loop(0, out.shape[0])
        def _(d):
            at = 2 * (side * out.shape[0] + d)
            first = panels[c][finals[at]].astype(jnp.float32)
            second = panels[c][finals[at + 1]].astype(jnp.float32)
            out[d, :, :, c * width : (c + 1) * width] = (first + second).astype(out.dtype)

    others = pl.ds(0, n - 1)
    others_near = pl.ds(0, half - 1)
    landed(left_send.at[others], left_out_sem)
    landed(a_send.at[others], a_out_sem)
    landed(lefts.at[parity], swap_out_sem)
    for c in range(chunks):
        landed(b_send.at[c, others], b_out_sem.at[c])
        landed(panels[c].at[others_near], result_out_sem.at[c])
        landed(relayed[c].at[others_near], relay_out_sem.at[c])
        landed(merged.at[c], far_out_sem.at[c])


def local(nodes, pair_nodes, prod_left, prod_right, prod_flag, prod_diag, *, n):
    _, parts, rows, order = nodes.shape
    count = prod_left.shape[0]
    assert count == n and rows * n == order
    half = diags = count // 2
    slots = half // 2 + 1
    chunks = order // TILE
    flags, merges, finals, left_send, a_send, b_send = plan_and_gather(
        nodes, pair_nodes, prod_left, prod_right, prod_flag, prod_diag, chunks
    )
    width = order // chunks
    kind = nodes.dtype
    dma = pltpu.SemaphoreType.DMA
    smem = pl.BlockSpec(memory_space=pltpu.SMEM)
    anywhere = pl.BlockSpec(memory_space=pl.ANY)
    return pl.pallas_call(
        functools.partial(exchange_kernel, n),
        out_shape=jax.ShapeDtypeStruct((diags, parts, rows, order), kind),
        in_specs=[smem, smem, smem, anywhere, anywhere, anywhere],
        out_specs=pl.BlockSpec(memory_space=pltpu.VMEM),
        scratch_shapes=[
            pltpu.VMEM((2, parts, order, order), kind),
            pltpu.VMEM((parts, order, order), kind),
            pltpu.VMEM((chunks, parts, order, width), kind),
            pltpu.VMEM((parts, order, order), kind),
            pltpu.VMEM((parts, order, order), kind),
            pltpu.VMEM((parts, order, width), kind),
            pltpu.VMEM((chunks, parts, order, width), kind),
            [pltpu.VMEM((half + slots + 1, parts, rows, width), kind)] * chunks,
            [pltpu.VMEM((half + 1, parts, rows, width), kind)] * chunks,
            pltpu.VMEM((chunks, slots, parts, rows, width), kind),
            dma,
            dma,
            dma((chunks,)),
            dma,
            dma((chunks,)),
            dma((chunks,)),
            dma((chunks,)),
            dma,
            dma,
            dma((chunks,)),
            dma,
            dma((chunks,)),
            dma((chunks,)),
            dma((chunks,)),
        ],
        compiler_params=pltpu.CompilerParams(
            collective_id=0, has_side_effects=True, vmem_limit_bytes=40 * 2**20
        ),
    )(flags, merges, finals, left_send, a_send, b_send)


def solution(mesh):
    placed = (P("grp", None, "node", None), P(), P(), P(), P(), P())
    return jax.shard_map(
        functools.partial(local, n=mesh.shape["node"]),
        mesh=mesh,
        in_specs=placed,
        out_specs=P("grp", None, "node", None),
        check_vma=False,
    )
```

```python
import functools

import jax
import jax.numpy as jnp
from jax import lax
from jax.experimental import pallas as pl
from jax.experimental.pallas import tpu as pltpu
from jax.sharding import PartitionSpec as P

TILE = 256


def plan_and_gather_kernel(
    pair_nodes,
    prod_left,
    prod_right,
    prod_flag,
    prod_diag,
    nodes,
    flags,
    merges,
    finals,
    left_out,
    a_out,
    b_out,
    seen_left,
    seen_diag,
    mate_left,
    mate_diag,
    done,
    slot_of,
    order,
    left_sem,
    a_sem,
    b_sem,
):
    count = prod_left.shape[0]
    diags = count // 2
    half = count // 2
    slots = half // 2 + 1
    chunks = b_out.shape[0]
    width = b_out.shape[-1]

    @pl.loop(0, pair_nodes.shape[0])
    def _(p):
        seen_left[p] = -1

    @pl.loop(0, diags)
    def _(d):
        seen_diag[d] = -1
        slot_of[d] = -1
        slot_of[diags + d] = -1

    @pl.loop(0, count)
    def _(k):
        done[k] = 0
        for group, seen, mate in (
            (prod_left[k], seen_left, mate_left),
            (prod_diag[k], seen_diag, mate_diag),
        ):
            earlier = seen[group]
            found = earlier >= 0
            mate[k] = earlier
            back = jnp.where(found, earlier, k)
            mate[back] = jnp.where(found, k, mate[back])
            seen[group] = k

    def place(g, now):
        other = mate_left[now]
        done[now] = 1
        done[other] = 1
        order[2 * g] = now
        order[2 * g + 1] = other
        for at, k in ((2 * g, now), (2 * g + 1, other)):
            flags[at] = prod_flag[k]
            left_id = pair_nodes[prod_left[k], at - 2 * g]
            right = prod_right[k]
            pltpu.make_async_copy(nodes.at[left_id], left_out.at[at], left_sem).start()
            pltpu.make_async_copy(nodes.at[pair_nodes[right, 0]], a_out.at[at], a_sem).start()
            for c in range(chunks):
                pltpu.make_async_copy(
                    nodes.at[pair_nodes[right, 1], :, :, pl.ds(c * width, width)],
                    b_out.at[c, at],
                    b_sem,
                ).start()
        free = lax.fori_loop(
            0,
            count,
            lambda k, best: jnp.where(done[count - 1 - k] == 0, count - 1 - k, best),
            jnp.int32(0),
        )
        follow = mate_diag[other]
        return jnp.where(done[follow] == 0, follow, free)

    lax.fori_loop(0, count // 2, place, jnp.int32(0))

    for h in range(2):
        base = h * slots

        @pl.loop(0, slots)
        def _(t):
            merges[2 * (base + t)] = half
            merges[2 * (base + t) + 1] = half

        def take(i, used):
            diag = prod_diag[order[h * half + i]]
            slot = slot_of[h * diags + diag]
            new = slot < 0
            slot = jnp.where(new, used, slot)
            slot_of[h * diags + diag] = slot
            at = 2 * (base + slot)
            merges[at] = jnp.where(new, i, merges[at])
            merges[at + 1] = jnp.where(new, half, i)
            return used + new.astype(jnp.int32)

        lax.fori_loop(0, half, take, jnp.int32(0))

    for h in range(2):

        @pl.loop(0, diags)
        def _(d):
            near = slot_of[h * diags + d]
            far = half + slot_of[(1 - h) * diags + d]
            here = near >= 0
            at = 2 * (h * slots + jnp.maximum(near, 0))
            both = here & (merges[at + 1] < half)
            finals[2 * (h * diags + d)] = jnp.where(here, merges[at], far)
            finals[2 * (h * diags + d) + 1] = jnp.where(
                both, merges[at + 1], jnp.where(here, far, half + slots)
            )

    pltpu.make_async_copy(left_out, left_out, left_sem).wait()
    pltpu.make_async_copy(a_out, a_out, a_sem).wait()
    pltpu.make_async_copy(b_out, b_out, b_sem).wait()


def plan_and_gather(nodes, pair_nodes, prod_left, prod_right, prod_flag, prod_diag, chunks):
    count = prod_left.shape[0]
    _, parts, rows, order = nodes.shape
    half = count // 2
    slots = half // 2 + 1
    whole = jax.ShapeDtypeStruct((count, parts, rows, order), nodes.dtype)
    cut = jax.ShapeDtypeStruct((chunks, count, parts, rows, order // chunks), nodes.dtype)
    table = lambda size: jax.ShapeDtypeStruct((size,), jnp.int32)
    smem = pl.BlockSpec(memory_space=pltpu.SMEM)
    scratch = lambda size: pltpu.SMEM((size,), jnp.int32)
    return pl.pallas_call(
        plan_and_gather_kernel,
        out_shape=(table(count), table(4 * slots), table(4 * half), whole, whole, cut),
        in_specs=[smem] * 5 + [pl.BlockSpec(memory_space=pltpu.HBM)],
        out_specs=[smem] * 3 + [pl.BlockSpec(memory_space=pltpu.VMEM)] * 3,
        scratch_shapes=[
            scratch(pair_nodes.shape[0]),
            scratch(half),
            scratch(count),
            scratch(count),
            scratch(count),
            scratch(2 * half),
            scratch(count),
            pltpu.SemaphoreType.DMA,
            pltpu.SemaphoreType.DMA,
            pltpu.SemaphoreType.DMA,
        ],
        compiler_params=pltpu.CompilerParams(vmem_limit_bytes=36 * 2**20),
    )(pair_nodes, prod_left, prod_right, prod_flag, prod_diag, nodes)


def tile_product(left_re, left_im, right_re, right_im):
    dot = functools.partial(jnp.dot, preferred_element_type=jnp.float32)
    real_part = dot(left_re, right_re) - dot(left_im, right_im)
    imag_part = dot(left_re, right_im) + dot(left_im, right_re)
    return real_part.astype(jnp.bfloat16), imag_part.astype(jnp.bfloat16)


def exchange_kernel(
    n,
    flags,
    merges,
    finals,
    left_send,
    a_send,
    b_send,
    out,
    lefts,
    a_full,
    b_full,
    left_plain,
    left_used,
    right_pair,
    result,
    panels,
    relayed,
    merged,
    left_sem,
    a_sem,
    b_sem,
    swap_sem,
    result_sem,
    relay_sem,
    far_sem,
    left_out_sem,
    a_out_sem,
    b_out_sem,
    swap_out_sem,
    result_out_sem,
    relay_out_sem,
    far_out_sem,
):
    me = lax.axis_index("node")
    parity = lax.rem(me, 2)
    partner = me + 1 - 2 * parity
    chunks = b_full.shape[0]
    order = a_full.shape[1]
    rows = left_send.shape[2]
    tiles = order // TILE
    my_rows = pl.ds(pl.multiple_of(me * rows, rows), rows)

    def target(t):
        half = lax.div(t + 1, 2)
        return lax.rem(me + n // 2 + (2 * lax.rem(t, 2) - 1) * half, n)

    barrier = pltpu.get_barrier_semaphore()

    @pl.loop(0, n - 1)
    def _(t):
        pl.semaphore_signal(
            barrier,
            inc=1,
            device_id={"node": target(t)},
            device_id_type=pl.DeviceIdType.MESH,
        )

    pl.semaphore_wait(barrier, n - 1)

    def push(src, dst, send_sem, recv_sem, to):
        pltpu.make_async_remote_copy(
            src_ref=src,
            dst_ref=dst,
            send_sem=send_sem,
            recv_sem=recv_sem,
            device_id={"node": to},
            device_id_type=pl.DeviceIdType.MESH,
        ).start()

    def landed(ref, sem):
        pltpu.make_async_copy(ref, ref, sem).wait()

    @pl.loop(0, n - 1)
    def _(t):
        to = target(t)
        push(left_send.at[to], lefts.at[lax.rem(to, 2), :, my_rows], left_out_sem, left_sem, to)

    pltpu.make_async_copy(left_send.at[me], lefts.at[parity, :, my_rows], left_sem).start()

    @pl.loop(0, n - 1)
    def _(t):
        to = target(t)
        push(a_send.at[to], a_full.at[:, my_rows], a_out_sem, a_sem, to)

    pltpu.make_async_copy(a_send.at[me], a_full.at[:, my_rows], a_sem).start()

    @pl.loop(0, chunks)
    def _(c):
        @pl.loop(0, n - 1)
        def _(t):
            to = target(t)
            push(b_send.at[c, to], b_full.at[c, :, my_rows], b_out_sem.at[c], b_sem.at[c], to)

        pltpu.make_async_copy(b_send.at[c, me], b_full.at[c, :, my_rows], b_sem.at[c]).start()

    landed(lefts.at[parity], left_sem)
    push(lefts.at[parity], lefts.at[parity], swap_out_sem, swap_sem, partner)
    landed(lefts.at[1 - parity], swap_sem)

    def block(i):
        return pl.ds(pl.multiple_of(i * TILE, TILE), TILE)

    @pl.loop(0, tiles * tiles)
    def _(t):
        down, across = block(lax.div(t, tiles)), block(lax.rem(t, tiles))
        real_part, imag_part = tile_product(
            lefts[0, 0, down, :], lefts[0, 1, down, :], lefts[1, 0, :, across], lefts[1, 1, :, across]
        )
        left_plain[0, down, across] = real_part
        left_plain[1, down, across] = imag_part

    half = n // 2
    slots = merged.shape[1]
    near, far = pl.ds(0, half), pl.ds(half, slots)
    side, place = lax.div(me, half), lax.rem(me, half)
    mirror = lax.rem(me + half, n)

    def rows_of(device):
        return pl.ds(pl.multiple_of(device * rows, rows), rows)

    for c in range(chunks):
        panels[c][half + slots] = jnp.zeros(panels[c].shape[1:], panels[c].dtype)
        relayed[c][half] = jnp.zeros(relayed[c].shape[1:], relayed[c].dtype)

    flipped = flags[me] == 1

    @pl.loop(0, tiles * tiles)
    def _(t):
        down, across = block(lax.div(t, tiles)), block(lax.rem(t, tiles))
        left_used[0, down, across] = jnp.where(
            flipped, left_plain[0, across, down].T, left_plain[0, down, across]
        )
        left_used[1, down, across] = jnp.where(
            flipped, -left_plain[1, across, down].T, left_plain[1, down, across]
        )

    landed(a_full, a_sem)

    def compute(c):
        landed(b_full.at[c], b_sem.at[c])

        @pl.loop(0, tiles)
        def _(i):
            down = block(i)
            real_part, imag_part = tile_product(
                a_full[0, down, :], a_full[1, down, :], b_full[c, 0], b_full[c, 1]
            )
            right_pair[0, down, :] = real_part
            right_pair[1, down, :] = imag_part

        @pl.loop(0, tiles)
        def _(i):
            down = block(i)
            real_part, imag_part = tile_product(
                left_used[0, down, :], left_used[1, down, :], right_pair[0], right_pair[1]
            )
            result[c, 0, down, :] = real_part
            result[c, 1, down, :] = imag_part

        @pl.loop(1, half)
        def _(t):
            to = side * half + lax.rem(place + t, half)
            push(
                result.at[c, :, rows_of(lax.rem(to + half, n))],
                relayed[c].at[place],
                relay_out_sem.at[c],
                relay_sem.at[c],
                to,
            )

        pltpu.make_async_copy(
            result.at[c, :, rows_of(mirror)], relayed[c].at[place], relay_sem.at[c]
        ).start()

        @pl.loop(1, half)
        def _(t):
            to = side * half + lax.rem(place + t, half)
            push(
                result.at[c, :, rows_of(to)],
                panels[c].at[place],
                result_out_sem.at[c],
                result_sem.at[c],
                to,
            )

        pltpu.make_async_copy(
            result.at[c, :, my_rows], panels[c].at[place], result_sem.at[c]
        ).start()

    def merge(c):
        landed(relayed[c].at[near], relay_sem.at[c])

        @pl.loop(0, slots)
        def _(t):
            at = 2 * (side * slots + t)
            first = relayed[c][merges[at]].astype(jnp.float32)
            second = relayed[c][merges[at + 1]].astype(jnp.float32)
            merged[c, t] = (first + second).astype(merged.dtype)

        push(merged.at[c], panels[c].at[far], far_out_sem.at[c], far_sem.at[c], mirror)

    for c in range(chunks):
        compute(c)
        if c > 0:
            merge(c - 1)
    merge(chunks - 1)

    width = b_full.shape[-1]
    for c in range(chunks):
        landed(panels[c].at[near], result_sem.at[c])
        landed(panels[c].at[far], far_sem.at[c])

        @pl.loop(0, out.shape[0])
        def _(d):
            at = 2 * (side * out.shape[0] + d)
            first = panels[c][finals[at]].astype(jnp.float32)
            second = panels[c][finals[at + 1]].astype(jnp.float32)
            out[d, :, :, c * width : (c + 1) * width] = (first + second).astype(out.dtype)

    others = pl.ds(0, n - 1)
    others_near = pl.ds(0, half - 1)
    landed(left_send.at[others], left_out_sem)
    landed(a_send.at[others], a_out_sem)
    landed(lefts.at[parity], swap_out_sem)
    for c in range(chunks):
        landed(b_send.at[c, others], b_out_sem.at[c])
        landed(panels[c].at[others_near], result_out_sem.at[c])
        landed(relayed[c].at[others_near], relay_out_sem.at[c])
        landed(merged.at[c], far_out_sem.at[c])


def local(nodes, pair_nodes, prod_left, prod_right, prod_flag, prod_diag, *, n):
    _, parts, rows, order = nodes.shape
    count = prod_left.shape[0]
    assert count == n and rows * n == order
    half = diags = count // 2
    slots = half // 2 + 1
    chunks = order // TILE
    flags, merges, finals, left_send, a_send, b_send = plan_and_gather(
        nodes, pair_nodes, prod_left, prod_right, prod_flag, prod_diag, chunks
    )
    width = order // chunks
    kind = nodes.dtype
    dma = pltpu.SemaphoreType.DMA
    smem = pl.BlockSpec(memory_space=pltpu.SMEM)
    anywhere = pl.BlockSpec(memory_space=pl.ANY)
    return pl.pallas_call(
        functools.partial(exchange_kernel, n),
        out_shape=jax.ShapeDtypeStruct((diags, parts, rows, order), kind),
        in_specs=[smem, smem, smem, anywhere, anywhere, anywhere],
        out_specs=pl.BlockSpec(memory_space=pltpu.VMEM),
        scratch_shapes=[
            pltpu.VMEM((2, parts, order, order), kind),
            pltpu.VMEM((parts, order, order), kind),
            pltpu.VMEM((chunks, parts, order, width), kind),
            pltpu.VMEM((parts, order, order), kind),
            pltpu.VMEM((parts, order, order), kind),
            pltpu.VMEM((parts, order, width), kind),
            pltpu.VMEM((chunks, parts, order, width), kind),
            [pltpu.VMEM((half + slots + 1, parts, rows, width), kind)] * chunks,
            [pltpu.VMEM((half + 1, parts, rows, width), kind)] * chunks,
            pltpu.VMEM((chunks, slots, parts, rows, width), kind),
            dma,
            dma,
            dma((chunks,)),
            dma,
            dma((chunks,)),
            dma((chunks,)),
            dma((chunks,)),
            dma,
            dma,
            dma((chunks,)),
            dma,
            dma((chunks,)),
            dma((chunks,)),
            dma((chunks,)),
        ],
        compiler_params=pltpu.CompilerParams(
            collective_id=0, has_side_effects=True, vmem_limit_bytes=38 * 2**20
        ),
    )(flags, merges, finals, left_send, a_send, b_send)


def solution(mesh):
    placed = (P("grp", None, "node", None), P(), P(), P(), P(), P())
    return jax.shard_map(
        functools.partial(local, n=mesh.shape["node"]),
        mesh=mesh,
        in_specs=placed,
        out_specs=P("grp", None, "node", None),
        check_vma=False,
    )
```

```python
import functools

import jax
import jax.numpy as jnp
from jax import lax
from jax.experimental import pallas as pl
from jax.experimental.pallas import tpu as pltpu
from jax.sharding import PartitionSpec as P

TILE = 256
AHEAD = 2


def plan_and_gather_kernel(
    graph,
    nodes,
    flags,
    merges,
    finals,
    left_out,
    a_out,
    b_out,
    seen_left,
    seen_diag,
    mate_left,
    mate_diag,
    done,
    slot_of,
    order,
    left_sem,
    a_sem,
    b_sem,
):
    count = graph.shape[1]
    diags = count // 2
    half = count // 2
    first_node, prod_left, prod_right, prod_flag, prod_diag = 0, 2, 3, 4, 5
    slots = half // 2 + 1
    chunks = b_out.shape[0]
    width = b_out.shape[-1]

    @pl.loop(0, count)
    def _(p):
        seen_left[p] = -1

    @pl.loop(0, diags)
    def _(d):
        seen_diag[d] = -1
        slot_of[d] = -1
        slot_of[diags + d] = -1

    @pl.loop(0, count)
    def _(k):
        done[k] = 0
        for group, seen, mate in (
            (graph[prod_left, k], seen_left, mate_left),
            (graph[prod_diag, k], seen_diag, mate_diag),
        ):
            earlier = seen[group]
            found = earlier >= 0
            mate[k] = earlier
            back = jnp.where(found, earlier, k)
            mate[back] = jnp.where(found, k, mate[back])
            seen[group] = k

    def place(g, now):
        other = mate_left[now]
        done[now] = 1
        done[other] = 1
        order[2 * g] = now
        order[2 * g + 1] = other
        for side, k in ((first_node, now), (first_node + 1, other)):
            at = 2 * g + side
            flags[at] = graph[prod_flag, k]
            left_id = graph[side, graph[prod_left, k]]
            right = graph[prod_right, k]
            pltpu.make_async_copy(nodes.at[left_id], left_out.at[at], left_sem).start()
            pltpu.make_async_copy(nodes.at[graph[first_node, right]], a_out.at[at], a_sem).start()
            for c in range(chunks):
                pltpu.make_async_copy(
                    nodes.at[graph[first_node + 1, right], :, :, pl.ds(c * width, width)],
                    b_out.at[c, at],
                    b_sem,
                ).start()
        free = lax.fori_loop(
            0,
            count,
            lambda k, best: jnp.where(done[count - 1 - k] == 0, count - 1 - k, best),
            jnp.int32(0),
            unroll=True,
        )
        follow = mate_diag[other]
        return jnp.where(done[follow] == 0, follow, free)

    lax.fori_loop(0, count // 2, place, jnp.int32(0))

    for h in range(2):
        base = h * slots

        @pl.loop(0, slots)
        def _(t):
            merges[2 * (base + t)] = half
            merges[2 * (base + t) + 1] = half

        def take(i, used):
            diag = graph[prod_diag, order[h * half + i]]
            slot = slot_of[h * diags + diag]
            new = slot < 0
            slot = jnp.where(new, used, slot)
            slot_of[h * diags + diag] = slot
            at = 2 * (base + slot)
            merges[at] = jnp.where(new, i, merges[at])
            merges[at + 1] = jnp.where(new, half, i)
            return used + new.astype(jnp.int32)

        lax.fori_loop(0, half, take, jnp.int32(0))

    for h in range(2):

        @pl.loop(0, diags)
        def _(d):
            near = slot_of[h * diags + d]
            far = half + slot_of[(1 - h) * diags + d]
            here = near >= 0
            at = 2 * (h * slots + jnp.maximum(near, 0))
            both = here & (merges[at + 1] < half)
            finals[2 * (h * diags + d)] = jnp.where(here, merges[at], far)
            finals[2 * (h * diags + d) + 1] = jnp.where(
                both, merges[at + 1], jnp.where(here, far, half + slots)
            )

    pltpu.make_async_copy(left_out, left_out, left_sem).wait()
    pltpu.make_async_copy(a_out, a_out, a_sem).wait()
    pltpu.make_async_copy(b_out, b_out, b_sem).wait()


def plan_and_gather(nodes, pair_nodes, prod_left, prod_right, prod_flag, prod_diag, chunks):
    count = prod_left.shape[0]
    _, parts, rows, order = nodes.shape
    half = count // 2
    slots = half // 2 + 1
    whole = jax.ShapeDtypeStruct((count, parts, rows, order), nodes.dtype)
    graph = jnp.stack(
        [pair_nodes[:, 0], pair_nodes[:, 1], prod_left, prod_right, prod_flag, prod_diag]
    )
    cut = jax.ShapeDtypeStruct((chunks, count, parts, rows, order // chunks), nodes.dtype)
    table = lambda size: jax.ShapeDtypeStruct((size,), jnp.int32)
    smem = pl.BlockSpec(memory_space=pltpu.SMEM)
    scratch = lambda size: pltpu.SMEM((size,), jnp.int32)
    return pl.pallas_call(
        plan_and_gather_kernel,
        out_shape=(table(count), table(4 * slots), table(4 * half), whole, whole, cut),
        in_specs=[smem, pl.BlockSpec(memory_space=pltpu.HBM)],
        out_specs=[smem] * 3 + [pl.BlockSpec(memory_space=pltpu.VMEM)] * 3,
        scratch_shapes=[
            scratch(count),
            scratch(half),
            scratch(count),
            scratch(count),
            scratch(count),
            scratch(2 * half),
            scratch(count),
            pltpu.SemaphoreType.DMA,
            pltpu.SemaphoreType.DMA,
            pltpu.SemaphoreType.DMA,
        ],
        compiler_params=pltpu.CompilerParams(vmem_limit_bytes=36 * 2**20),
    )(graph, nodes)


def tile_product(left_re, left_im, right_re, right_im):
    dot = functools.partial(jnp.dot, preferred_element_type=jnp.float32)
    real_part = dot(left_re, right_re) - dot(left_im, right_im)
    imag_part = dot(left_re, right_im) + dot(left_im, right_re)
    return real_part.astype(jnp.bfloat16), imag_part.astype(jnp.bfloat16)


def exchange_kernel(
    n,
    flags,
    merges,
    finals,
    left_send,
    a_send,
    b_send,
    out,
    lefts,
    a_full,
    b_full,
    left_plain,
    left_used,
    right_pair,
    result,
    panels,
    relayed,
    merged,
    left_sem,
    a_sem,
    b_sem,
    swap_sem,
    result_sem,
    relay_sem,
    far_sem,
    left_out_sem,
    a_out_sem,
    b_out_sem,
    swap_out_sem,
    result_out_sem,
    relay_out_sem,
    far_out_sem,
):
    me = lax.axis_index("node")
    parity = lax.rem(me, 2)
    partner = me + 1 - 2 * parity
    chunks = b_full.shape[0]
    order = a_full.shape[1]
    rows = left_send.shape[2]
    tiles = order // TILE
    my_rows = pl.ds(pl.multiple_of(me * rows, rows), rows)

    def target(t):
        half = lax.div(t + 1, 2)
        return lax.rem(me + n // 2 + (2 * lax.rem(t, 2) - 1) * half, n)

    barrier = pltpu.get_barrier_semaphore()

    @pl.loop(0, n - 1)
    def _(t):
        pl.semaphore_signal(
            barrier,
            inc=1,
            device_id={"node": target(t)},
            device_id_type=pl.DeviceIdType.MESH,
        )

    pl.semaphore_wait(barrier, n - 1)

    def push(src, dst, send_sem, recv_sem, to):
        pltpu.make_async_remote_copy(
            src_ref=src,
            dst_ref=dst,
            send_sem=send_sem,
            recv_sem=recv_sem,
            device_id={"node": to},
            device_id_type=pl.DeviceIdType.MESH,
        ).start()

    def landed(ref, sem):
        pltpu.make_async_copy(ref, ref, sem).wait()

    @pl.loop(0, n - 1)
    def _(t):
        to = target(t)
        push(left_send.at[to], lefts.at[lax.rem(to, 2), :, my_rows], left_out_sem, left_sem, to)

    pltpu.make_async_copy(left_send.at[me], lefts.at[parity, :, my_rows], left_sem).start()

    @pl.loop(0, n - 1)
    def _(t):
        to = target(t)
        push(a_send.at[to], a_full.at[:, my_rows], a_out_sem, a_sem, to)

    pltpu.make_async_copy(a_send.at[me], a_full.at[:, my_rows], a_sem).start()

    def push_right(c):
        @pl.loop(0, n - 1)
        def _(t):
            to = target(t)
            push(b_send.at[c, to], b_full.at[c, :, my_rows], b_out_sem.at[c], b_sem.at[c], to)

        pltpu.make_async_copy(b_send.at[c, me], b_full.at[c, :, my_rows], b_sem.at[c]).start()

    for c in range(min(AHEAD, chunks)):
        push_right(c)

    landed(lefts.at[parity], left_sem)
    push(lefts.at[parity], lefts.at[parity], swap_out_sem, swap_sem, partner)
    landed(lefts.at[1 - parity], swap_sem)

    def block(i):
        return pl.ds(pl.multiple_of(i * TILE, TILE), TILE)

    @pl.loop(0, tiles * tiles)
    def _(t):
        down, across = block(lax.div(t, tiles)), block(lax.rem(t, tiles))
        real_part, imag_part = tile_product(
            lefts[0, 0, down, :], lefts[0, 1, down, :], lefts[1, 0, :, across], lefts[1, 1, :, across]
        )
        left_plain[0, down, across] = real_part
        left_plain[1, down, across] = imag_part

    half = n // 2
    slots = merged.shape[1]
    near, far = pl.ds(0, half), pl.ds(half, slots)
    side, place = lax.div(me, half), lax.rem(me, half)
    mirror = lax.rem(me + half, n)

    def rows_of(device):
        return pl.ds(pl.multiple_of(device * rows, rows), rows)

    for c in range(chunks):
        panels[c][half + slots] = jnp.zeros(panels[c].shape[1:], panels[c].dtype)
        relayed[c][half] = jnp.zeros(relayed[c].shape[1:], relayed[c].dtype)

    flipped = flags[me] == 1

    @pl.loop(0, tiles * tiles)
    def _(t):
        down, across = block(lax.div(t, tiles)), block(lax.rem(t, tiles))
        left_used[0, down, across] = jnp.where(
            flipped, left_plain[0, across, down].T, left_plain[0, down, across]
        )
        left_used[1, down, across] = jnp.where(
            flipped, -left_plain[1, across, down].T, left_plain[1, down, across]
        )

    landed(a_full, a_sem)

    def compute(c):
        landed(b_full.at[c], b_sem.at[c])

        @pl.loop(0, tiles)
        def _(i):
            down = block(i)
            real_part, imag_part = tile_product(
                a_full[0, down, :], a_full[1, down, :], b_full[c, 0], b_full[c, 1]
            )
            right_pair[0, down, :] = real_part
            right_pair[1, down, :] = imag_part

        @pl.loop(0, tiles)
        def _(i):
            down = block(i)
            real_part, imag_part = tile_product(
                left_used[0, down, :], left_used[1, down, :], right_pair[0], right_pair[1]
            )
            result[c, 0, down, :] = real_part
            result[c, 1, down, :] = imag_part

        @pl.loop(1, half)
        def _(t):
            to = side * half + lax.rem(place + t, half)
            push(
                result.at[c, :, rows_of(lax.rem(to + half, n))],
                relayed[c].at[place],
                relay_out_sem.at[c],
                relay_sem.at[c],
                to,
            )

        pltpu.make_async_copy(
            result.at[c, :, rows_of(mirror)], relayed[c].at[place], relay_sem.at[c]
        ).start()

        @pl.loop(1, half)
        def _(t):
            to = side * half + lax.rem(place + t, half)
            push(
                result.at[c, :, rows_of(to)],
                panels[c].at[place],
                result_out_sem.at[c],
                result_sem.at[c],
                to,
            )

        pltpu.make_async_copy(
            result.at[c, :, my_rows], panels[c].at[place], result_sem.at[c]
        ).start()

    def merge(c):
        landed(relayed[c].at[near], relay_sem.at[c])

        @pl.loop(0, slots)
        def _(t):
            at = 2 * (side * slots + t)
            first = relayed[c][merges[at]].astype(jnp.float32)
            second = relayed[c][merges[at + 1]].astype(jnp.float32)
            merged[c, t] = (first + second).astype(merged.dtype)

        push(merged.at[c], panels[c].at[far], far_out_sem.at[c], far_sem.at[c], mirror)

    for c in range(chunks):
        compute(c)
        if c + AHEAD < chunks:
            push_right(c + AHEAD)
        if c > 0:
            merge(c - 1)
    merge(chunks - 1)

    width = b_full.shape[-1]
    for c in range(chunks):
        landed(panels[c].at[near], result_sem.at[c])
        landed(panels[c].at[far], far_sem.at[c])

        @pl.loop(0, out.shape[0])
        def _(d):
            at = 2 * (side * out.shape[0] + d)
            first = panels[c][finals[at]].astype(jnp.float32)
            second = panels[c][finals[at + 1]].astype(jnp.float32)
            out[d, :, :, c * width : (c + 1) * width] = (first + second).astype(out.dtype)

    others = pl.ds(0, n - 1)
    others_near = pl.ds(0, half - 1)
    landed(left_send.at[others], left_out_sem)
    landed(a_send.at[others], a_out_sem)
    landed(lefts.at[parity], swap_out_sem)
    for c in range(chunks):
        landed(b_send.at[c, others], b_out_sem.at[c])
        landed(panels[c].at[others_near], result_out_sem.at[c])
        landed(relayed[c].at[others_near], relay_out_sem.at[c])
        landed(merged.at[c], far_out_sem.at[c])


def local(nodes, pair_nodes, prod_left, prod_right, prod_flag, prod_diag, *, n):
    _, parts, rows, order = nodes.shape
    count = prod_left.shape[0]
    assert count == n == pair_nodes.shape[0] and rows * n == order
    half = diags = count // 2
    slots = half // 2 + 1
    chunks = order // TILE
    flags, merges, finals, left_send, a_send, b_send = plan_and_gather(
        nodes, pair_nodes, prod_left, prod_right, prod_flag, prod_diag, chunks
    )
    width = order // chunks
    kind = nodes.dtype
    dma = pltpu.SemaphoreType.DMA
    smem = pl.BlockSpec(memory_space=pltpu.SMEM)
    anywhere = pl.BlockSpec(memory_space=pl.ANY)
    return pl.pallas_call(
        functools.partial(exchange_kernel, n),
        out_shape=jax.ShapeDtypeStruct((diags, parts, rows, order), kind),
        in_specs=[smem, smem, smem, anywhere, anywhere, anywhere],
        out_specs=pl.BlockSpec(memory_space=pltpu.VMEM),
        scratch_shapes=[
            pltpu.VMEM((2, parts, order, order), kind),
            pltpu.VMEM((parts, order, order), kind),
            pltpu.VMEM((chunks, parts, order, width), kind),
            pltpu.VMEM((parts, order, order), kind),
            pltpu.VMEM((parts, order, order), kind),
            pltpu.VMEM((parts, order, width), kind),
            pltpu.VMEM((chunks, parts, order, width), kind),
            [pltpu.VMEM((half + slots + 1, parts, rows, width), kind)] * chunks,
            [pltpu.VMEM((half + 1, parts, rows, width), kind)] * chunks,
            pltpu.VMEM((chunks, slots, parts, rows, width), kind),
            dma,
            dma,
            dma((chunks,)),
            dma,
            dma((chunks,)),
            dma((chunks,)),
            dma((chunks,)),
            dma,
            dma,
            dma((chunks,)),
            dma,
            dma((chunks,)),
            dma((chunks,)),
            dma((chunks,)),
        ],
        compiler_params=pltpu.CompilerParams(
            collective_id=0, has_side_effects=True, vmem_limit_bytes=38 * 2**20
        ),
    )(flags, merges, finals, left_send, a_send, b_send)


def solution(mesh):
    placed = (P("grp", None, "node", None), P(), P(), P(), P(), P())
    return jax.shard_map(
        functools.partial(local, n=mesh.shape["node"]),
        mesh=mesh,
        in_specs=placed,
        out_specs=P("grp", None, "node", None),
        check_vma=False,
    )
```

```python
import functools

import jax
import jax.numpy as jnp
from jax import lax
from jax.experimental import pallas as pl
from jax.experimental.pallas import tpu as pltpu
from jax.sharding import PartitionSpec as P

TILE = 256
AHEAD = 2


def plan_and_gather_kernel(
    graph,
    nodes,
    flags,
    merges,
    finals,
    left_out,
    a_out,
    b_out,
    seen_left,
    seen_diag,
    mate_left,
    mate_diag,
    done,
    slot_of,
    order,
    left_sem,
    a_sem,
    b_sem,
):
    count = graph.shape[1]
    diags = count // 2
    half = count // 2
    first_node, prod_left, prod_right, prod_flag, prod_diag = 0, 2, 3, 4, 5
    slots = half // 2 + 1

    @pl.loop(0, count)
    def _(p):
        seen_left[p] = -1

    @pl.loop(0, diags)
    def _(d):
        seen_diag[d] = -1
        slot_of[d] = -1
        slot_of[diags + d] = -1

    @pl.loop(0, count)
    def _(k):
        done[k] = 0
        for group, seen, mate in (
            (graph[prod_left, k], seen_left, mate_left),
            (graph[prod_diag, k], seen_diag, mate_diag),
        ):
            earlier = seen[group]
            found = earlier >= 0
            mate[k] = earlier
            back = jnp.where(found, earlier, k)
            mate[back] = jnp.where(found, k, mate[back])
            seen[group] = k

    def place(g, now):
        other = mate_left[now]
        done[now] = 1
        done[other] = 1
        order[2 * g] = now
        order[2 * g + 1] = other
        for side, k in ((first_node, now), (first_node + 1, other)):
            at = 2 * g + side
            flags[at] = graph[prod_flag, k]
            left_id = graph[side, graph[prod_left, k]]
            right = graph[prod_right, k]
            pltpu.make_async_copy(nodes.at[left_id], left_out.at[at], left_sem).start()
            pltpu.make_async_copy(nodes.at[graph[first_node, right]], a_out.at[at], a_sem).start()
            pltpu.make_async_copy(
                nodes.at[graph[first_node + 1, right]], b_out.at[at], b_sem
            ).start()
        free = lax.fori_loop(
            0,
            count,
            lambda k, best: jnp.where(done[count - 1 - k] == 0, count - 1 - k, best),
            jnp.int32(0),
            unroll=True,
        )
        follow = mate_diag[other]
        return jnp.where(done[follow] == 0, follow, free)

    lax.fori_loop(0, count // 2, place, jnp.int32(0))

    for h in range(2):
        base = h * slots

        @pl.loop(0, slots)
        def _(t):
            merges[2 * (base + t)] = half
            merges[2 * (base + t) + 1] = half

        def take(i, used):
            diag = graph[prod_diag, order[h * half + i]]
            slot = slot_of[h * diags + diag]
            new = slot < 0
            slot = jnp.where(new, used, slot)
            slot_of[h * diags + diag] = slot
            at = 2 * (base + slot)
            merges[at] = jnp.where(new, i, merges[at])
            merges[at + 1] = jnp.where(new, half, i)
            return used + new.astype(jnp.int32)

        lax.fori_loop(0, half, take, jnp.int32(0))

    for h in range(2):

        @pl.loop(0, diags)
        def _(d):
            near = slot_of[h * diags + d]
            far = half + slot_of[(1 - h) * diags + d]
            here = near >= 0
            at = 2 * (h * slots + jnp.maximum(near, 0))
            both = here & (merges[at + 1] < half)
            finals[2 * (h * diags + d)] = jnp.where(here, merges[at], far)
            finals[2 * (h * diags + d) + 1] = jnp.where(
                both, merges[at + 1], jnp.where(here, far, half + slots)
            )

    pltpu.make_async_copy(left_out, left_out, left_sem).wait()
    pltpu.make_async_copy(a_out, a_out, a_sem).wait()
    pltpu.make_async_copy(b_out, b_out, b_sem).wait()


def plan_and_gather(nodes, pair_nodes, prod_left, prod_right, prod_flag, prod_diag):
    count = prod_left.shape[0]
    _, parts, rows, order = nodes.shape
    half = count // 2
    slots = half // 2 + 1
    whole = jax.ShapeDtypeStruct((count, parts, rows, order), nodes.dtype)
    graph = jnp.stack(
        [pair_nodes[:, 0], pair_nodes[:, 1], prod_left, prod_right, prod_flag, prod_diag]
    )
    table = lambda size: jax.ShapeDtypeStruct((size,), jnp.int32)
    smem = pl.BlockSpec(memory_space=pltpu.SMEM)
    scratch = lambda size: pltpu.SMEM((size,), jnp.int32)
    return pl.pallas_call(
        plan_and_gather_kernel,
        out_shape=(table(count), table(4 * slots), table(4 * half), whole, whole, whole),
        in_specs=[smem, pl.BlockSpec(memory_space=pltpu.HBM)],
        out_specs=[smem] * 3 + [pl.BlockSpec(memory_space=pltpu.VMEM)] * 3,
        scratch_shapes=[
            scratch(count),
            scratch(half),
            scratch(count),
            scratch(count),
            scratch(count),
            scratch(2 * half),
            scratch(count),
            pltpu.SemaphoreType.DMA,
            pltpu.SemaphoreType.DMA,
            pltpu.SemaphoreType.DMA,
        ],
        compiler_params=pltpu.CompilerParams(vmem_limit_bytes=36 * 2**20),
    )(graph, nodes)


def tile_product(left_re, left_im, right_re, right_im):
    dot = functools.partial(jnp.dot, preferred_element_type=jnp.float32)
    real_part = dot(left_re, right_re) - dot(left_im, right_im)
    imag_part = dot(left_re, right_im) + dot(left_im, right_re)
    return real_part.astype(jnp.bfloat16), imag_part.astype(jnp.bfloat16)


def exchange_kernel(
    n,
    flags,
    merges,
    finals,
    left_send,
    a_send,
    b_send,
    out,
    lefts,
    a_full,
    b_full,
    left_plain,
    left_used,
    right_pair,
    result,
    panels,
    relayed,
    merged,
    left_sem,
    a_sem,
    b_sem,
    swap_sem,
    result_sem,
    relay_sem,
    far_sem,
    left_out_sem,
    a_out_sem,
    b_out_sem,
    swap_out_sem,
    result_out_sem,
    relay_out_sem,
    far_out_sem,
):
    me = lax.axis_index("node")
    parity = lax.rem(me, 2)
    partner = me + 1 - 2 * parity
    chunks = b_full.shape[0]
    order = a_full.shape[1]
    rows = left_send.shape[2]
    tiles = order // TILE
    my_rows = pl.ds(pl.multiple_of(me * rows, rows), rows)

    def target(t):
        half = lax.div(t + 1, 2)
        return lax.rem(me + n // 2 + (2 * lax.rem(t, 2) - 1) * half, n)

    barrier = pltpu.get_barrier_semaphore()

    @pl.loop(0, n - 1)
    def _(t):
        pl.semaphore_signal(
            barrier,
            inc=1,
            device_id={"node": target(t)},
            device_id_type=pl.DeviceIdType.MESH,
        )

    pl.semaphore_wait(barrier, n - 1)

    def push(src, dst, send_sem, recv_sem, to):
        pltpu.make_async_remote_copy(
            src_ref=src,
            dst_ref=dst,
            send_sem=send_sem,
            recv_sem=recv_sem,
            device_id={"node": to},
            device_id_type=pl.DeviceIdType.MESH,
        ).start()

    def landed(ref, sem):
        pltpu.make_async_copy(ref, ref, sem).wait()

    @pl.loop(0, n - 1)
    def _(t):
        to = target(t)
        push(left_send.at[to], lefts.at[lax.rem(to, 2), :, my_rows], left_out_sem, left_sem, to)

    pltpu.make_async_copy(left_send.at[me], lefts.at[parity, :, my_rows], left_sem).start()

    @pl.loop(0, n - 1)
    def _(t):
        to = target(t)
        push(a_send.at[to], a_full.at[:, my_rows], a_out_sem, a_sem, to)

    pltpu.make_async_copy(a_send.at[me], a_full.at[:, my_rows], a_sem).start()

    def push_right(c):
        columns = pl.ds(c * b_full.shape[-1], b_full.shape[-1])

        @pl.loop(0, n - 1)
        def _(t):
            to = target(t)
            push(b_send.at[to, :, :, columns], b_full.at[c, :, my_rows], b_out_sem.at[c], b_sem.at[c], to)

        pltpu.make_async_copy(
            b_send.at[me, :, :, columns], b_full.at[c, :, my_rows], b_sem.at[c]
        ).start()

    for c in range(min(AHEAD, chunks)):
        push_right(c)

    landed(lefts.at[parity], left_sem)
    push(lefts.at[parity], lefts.at[parity], swap_out_sem, swap_sem, partner)
    landed(lefts.at[1 - parity], swap_sem)

    def block(i):
        return pl.ds(pl.multiple_of(i * TILE, TILE), TILE)

    @pl.loop(0, tiles * tiles)
    def _(t):
        down, across = block(lax.div(t, tiles)), block(lax.rem(t, tiles))
        real_part, imag_part = tile_product(
            lefts[0, 0, down, :], lefts[0, 1, down, :], lefts[1, 0, :, across], lefts[1, 1, :, across]
        )
        left_plain[0, down, across] = real_part
        left_plain[1, down, across] = imag_part

    half = n // 2
    slots = merged.shape[1]
    near, far = pl.ds(0, half), pl.ds(half, slots)
    side, place = lax.div(me, half), lax.rem(me, half)
    mirror = lax.rem(me + half, n)

    def rows_of(device):
        return pl.ds(pl.multiple_of(device * rows, rows), rows)

    for c in range(chunks):
        panels[c][half + slots] = jnp.zeros(panels[c].shape[1:], panels[c].dtype)
        relayed[c][half] = jnp.zeros(relayed[c].shape[1:], relayed[c].dtype)

    flipped = flags[me] == 1

    @pl.loop(0, tiles * tiles)
    def _(t):
        down, across = block(lax.div(t, tiles)), block(lax.rem(t, tiles))
        left_used[0, down, across] = jnp.where(
            flipped, left_plain[0, across, down].T, left_plain[0, down, across]
        )
        left_used[1, down, across] = jnp.where(
            flipped, -left_plain[1, across, down].T, left_plain[1, down, across]
        )

    landed(a_full, a_sem)

    def compute(c):
        landed(b_full.at[c], b_sem.at[c])

        @pl.loop(0, tiles)
        def _(i):
            down = block(i)
            real_part, imag_part = tile_product(
                a_full[0, down, :], a_full[1, down, :], b_full[c, 0], b_full[c, 1]
            )
            right_pair[0, down, :] = real_part
            right_pair[1, down, :] = imag_part

        @pl.loop(0, tiles)
        def _(i):
            down = block(i)
            real_part, imag_part = tile_product(
                left_used[0, down, :], left_used[1, down, :], right_pair[0], right_pair[1]
            )
            result[c, 0, down, :] = real_part
            result[c, 1, down, :] = imag_part

        @pl.loop(1, half)
        def _(t):
            to = side * half + lax.rem(place + t, half)
            push(
                result.at[c, :, rows_of(lax.rem(to + half, n))],
                relayed[c].at[place],
                relay_out_sem.at[c],
                relay_sem.at[c],
                to,
            )

        pltpu.make_async_copy(
            result.at[c, :, rows_of(mirror)], relayed[c].at[place], relay_sem.at[c]
        ).start()

        @pl.loop(1, half)
        def _(t):
            to = side * half + lax.rem(place + t, half)
            push(
                result.at[c, :, rows_of(to)],
                panels[c].at[place],
                result_out_sem.at[c],
                result_sem.at[c],
                to,
            )

        pltpu.make_async_copy(
            result.at[c, :, my_rows], panels[c].at[place], result_sem.at[c]
        ).start()

    def merge(c):
        landed(relayed[c].at[near], relay_sem.at[c])

        @pl.loop(0, slots)
        def _(t):
            at = 2 * (side * slots + t)
            first = relayed[c][merges[at]].astype(jnp.float32)
            second = relayed[c][merges[at + 1]].astype(jnp.float32)
            merged[c, t] = (first + second).astype(merged.dtype)

        push(merged.at[c], panels[c].at[far], far_out_sem.at[c], far_sem.at[c], mirror)

    for c in range(chunks):
        compute(c)
        if c + AHEAD < chunks:
            push_right(c + AHEAD)
        if c > 0:
            merge(c - 1)
    merge(chunks - 1)

    width = b_full.shape[-1]
    for c in range(chunks):
        landed(panels[c].at[near], result_sem.at[c])
        landed(panels[c].at[far], far_sem.at[c])

        @pl.loop(0, out.shape[0])
        def _(d):
            at = 2 * (side * out.shape[0] + d)
            first = panels[c][finals[at]].astype(jnp.float32)
            second = panels[c][finals[at + 1]].astype(jnp.float32)
            out[d, :, :, c * width : (c + 1) * width] = (first + second).astype(out.dtype)

    others, sent_rows = pl.ds(0, n - 1), pl.ds(0, (n - 1) * rows)
    others_near = pl.ds(0, half - 1)
    landed(left_send.at[others], left_out_sem)
    landed(a_send.at[others], a_out_sem)
    landed(lefts.at[parity], swap_out_sem)
    for c in range(chunks):
        landed(b_full.at[c, :, sent_rows], b_out_sem.at[c])
        landed(panels[c].at[others_near], result_out_sem.at[c])
        landed(relayed[c].at[others_near], relay_out_sem.at[c])
        landed(merged.at[c], far_out_sem.at[c])


def local(nodes, pair_nodes, prod_left, prod_right, prod_flag, prod_diag, *, n):
    _, parts, rows, order = nodes.shape
    count = prod_left.shape[0]
    assert count == n == pair_nodes.shape[0] and rows * n == order
    half = diags = count // 2
    slots = half // 2 + 1
    chunks = order // TILE
    flags, merges, finals, left_send, a_send, b_send = plan_and_gather(
        nodes, pair_nodes, prod_left, prod_right, prod_flag, prod_diag
    )
    width = order // chunks
    kind = nodes.dtype
    dma = pltpu.SemaphoreType.DMA
    smem = pl.BlockSpec(memory_space=pltpu.SMEM)
    anywhere = pl.BlockSpec(memory_space=pl.ANY)
    return pl.pallas_call(
        functools.partial(exchange_kernel, n),
        out_shape=jax.ShapeDtypeStruct((diags, parts, rows, order), kind),
        in_specs=[smem, smem, smem, anywhere, anywhere, anywhere],
        out_specs=pl.BlockSpec(memory_space=pltpu.VMEM),
        scratch_shapes=[
            pltpu.VMEM((2, parts, order, order), kind),
            pltpu.VMEM((parts, order, order), kind),
            pltpu.VMEM((chunks, parts, order, width), kind),
            pltpu.VMEM((parts, order, order), kind),
            pltpu.VMEM((parts, order, order), kind),
            pltpu.VMEM((parts, order, width), kind),
            pltpu.VMEM((chunks, parts, order, width), kind),
            [pltpu.VMEM((half + slots + 1, parts, rows, width), kind)] * chunks,
            [pltpu.VMEM((half + 1, parts, rows, width), kind)] * chunks,
            pltpu.VMEM((chunks, slots, parts, rows, width), kind),
            dma,
            dma,
            dma((chunks,)),
            dma,
            dma((chunks,)),
            dma((chunks,)),
            dma((chunks,)),
            dma,
            dma,
            dma((chunks,)),
            dma,
            dma((chunks,)),
            dma((chunks,)),
            dma((chunks,)),
        ],
        compiler_params=pltpu.CompilerParams(
            collective_id=0, has_side_effects=True, vmem_limit_bytes=38 * 2**20
        ),
    )(flags, merges, finals, left_send, a_send, b_send)


def solution(mesh):
    placed = (P("grp", None, "node", None), P(), P(), P(), P(), P())
    return jax.shard_map(
        functools.partial(local, n=mesh.shape["node"]),
        mesh=mesh,
        in_specs=placed,
        out_specs=P("grp", None, "node", None),
        check_vma=False,
    )
```

```python
import functools

import jax
import jax.numpy as jnp
from jax import lax
from jax.experimental import pallas as pl
from jax.experimental.pallas import tpu as pltpu
from jax.sharding import PartitionSpec as P

TILE = 256
AHEAD = 4
WIDTH = 128


def plan_and_gather_kernel(
    graph,
    nodes,
    flags,
    merges,
    finals,
    left_out,
    a_out,
    b_out,
    seen_left,
    seen_diag,
    mate_left,
    mate_diag,
    done,
    slot_of,
    order,
    left_sem,
    a_sem,
    b_sem,
):
    count = graph.shape[1]
    diags = count // 2
    half = count // 2
    first_node, prod_left, prod_right, prod_flag, prod_diag = 0, 2, 3, 4, 5
    slots = half // 2 + 1
    chunks = b_out.shape[0]
    width = b_out.shape[-1]

    @pl.loop(0, count)
    def _(p):
        seen_left[p] = -1

    @pl.loop(0, diags)
    def _(d):
        seen_diag[d] = -1
        slot_of[d] = -1
        slot_of[diags + d] = -1

    @pl.loop(0, count)
    def _(k):
        done[k] = 0
        for group, seen, mate in (
            (graph[prod_left, k], seen_left, mate_left),
            (graph[prod_diag, k], seen_diag, mate_diag),
        ):
            earlier = seen[group]
            found = earlier >= 0
            mate[k] = earlier
            back = jnp.where(found, earlier, k)
            mate[back] = jnp.where(found, k, mate[back])
            seen[group] = k

    def place(g, now):
        other = mate_left[now]
        done[now] = 1
        done[other] = 1
        order[2 * g] = now
        order[2 * g + 1] = other
        for side, k in ((first_node, now), (first_node + 1, other)):
            at = 2 * g + side
            flags[at] = graph[prod_flag, k]
            left_id = graph[side, graph[prod_left, k]]
            right = graph[prod_right, k]
            pltpu.make_async_copy(nodes.at[left_id], left_out.at[at], left_sem).start()
            pltpu.make_async_copy(nodes.at[graph[first_node, right]], a_out.at[at], a_sem).start()
            for c in range(chunks):
                pltpu.make_async_copy(
                    nodes.at[graph[first_node + 1, right], :, :, pl.ds(c * width, width)],
                    b_out.at[c, at],
                    b_sem,
                ).start()
        free = lax.fori_loop(
            0,
            count,
            lambda k, best: jnp.where(done[count - 1 - k] == 0, count - 1 - k, best),
            jnp.int32(0),
            unroll=True,
        )
        follow = mate_diag[other]
        return jnp.where(done[follow] == 0, follow, free)

    lax.fori_loop(0, count // 2, place, jnp.int32(0))

    for h in range(2):
        base = h * slots

        @pl.loop(0, slots)
        def _(t):
            merges[2 * (base + t)] = half
            merges[2 * (base + t) + 1] = half

        def take(i, used):
            diag = graph[prod_diag, order[h * half + i]]
            slot = slot_of[h * diags + diag]
            new = slot < 0
            slot = jnp.where(new, used, slot)
            slot_of[h * diags + diag] = slot
            at = 2 * (base + slot)
            merges[at] = jnp.where(new, i, merges[at])
            merges[at + 1] = jnp.where(new, half, i)
            return used + new.astype(jnp.int32)

        lax.fori_loop(0, half, take, jnp.int32(0))

    for h in range(2):

        @pl.loop(0, diags)
        def _(d):
            near = slot_of[h * diags + d]
            far = half + slot_of[(1 - h) * diags + d]
            here = near >= 0
            at = 2 * (h * slots + jnp.maximum(near, 0))
            both = here & (merges[at + 1] < half)
            finals[2 * (h * diags + d)] = jnp.where(here, merges[at], far)
            finals[2 * (h * diags + d) + 1] = jnp.where(
                both, merges[at + 1], jnp.where(here, far, half + slots)
            )

    pltpu.make_async_copy(left_out, left_out, left_sem).wait()
    pltpu.make_async_copy(a_out, a_out, a_sem).wait()
    pltpu.make_async_copy(b_out, b_out, b_sem).wait()


def plan_and_gather(nodes, pair_nodes, prod_left, prod_right, prod_flag, prod_diag, chunks):
    count = prod_left.shape[0]
    _, parts, rows, order = nodes.shape
    half = count // 2
    slots = half // 2 + 1
    whole = jax.ShapeDtypeStruct((count, parts, rows, order), nodes.dtype)
    graph = jnp.stack(
        [pair_nodes[:, 0], pair_nodes[:, 1], prod_left, prod_right, prod_flag, prod_diag]
    )
    cut = jax.ShapeDtypeStruct((chunks, count, parts, rows, order // chunks), nodes.dtype)
    table = lambda size: jax.ShapeDtypeStruct((size,), jnp.int32)
    smem = pl.BlockSpec(memory_space=pltpu.SMEM)
    scratch = lambda size: pltpu.SMEM((size,), jnp.int32)
    return pl.pallas_call(
        plan_and_gather_kernel,
        out_shape=(table(count), table(4 * slots), table(4 * half), whole, whole, cut),
        in_specs=[smem, pl.BlockSpec(memory_space=pltpu.HBM)],
        out_specs=[smem] * 3 + [pl.BlockSpec(memory_space=pltpu.VMEM)] * 3,
        scratch_shapes=[
            scratch(count),
            scratch(half),
            scratch(count),
            scratch(count),
            scratch(count),
            scratch(2 * half),
            scratch(count),
            pltpu.SemaphoreType.DMA,
            pltpu.SemaphoreType.DMA,
            pltpu.SemaphoreType.DMA,
        ],
        compiler_params=pltpu.CompilerParams(vmem_limit_bytes=36 * 2**20),
    )(graph, nodes)


def tile_product(left_re, left_im, right_re, right_im):
    dot = functools.partial(jnp.dot, preferred_element_type=jnp.float32)
    real_part = dot(left_re, right_re) - dot(left_im, right_im)
    imag_part = dot(left_re, right_im) + dot(left_im, right_re)
    return real_part.astype(jnp.bfloat16), imag_part.astype(jnp.bfloat16)


def exchange_kernel(
    n,
    flags,
    merges,
    finals,
    left_send,
    a_send,
    b_send,
    out,
    lefts,
    a_full,
    b_full,
    left_plain,
    left_used,
    right_pair,
    result,
    panels,
    relayed,
    merged,
    left_sem,
    a_sem,
    b_sem,
    swap_sem,
    result_sem,
    relay_sem,
    far_sem,
    left_out_sem,
    a_out_sem,
    b_out_sem,
    swap_out_sem,
    result_out_sem,
    relay_out_sem,
    far_out_sem,
):
    me = lax.axis_index("node")
    parity = lax.rem(me, 2)
    partner = me + 1 - 2 * parity
    chunks = b_full.shape[0]
    order = a_full.shape[1]
    rows = left_send.shape[2]
    tiles = order // TILE
    my_rows = pl.ds(pl.multiple_of(me * rows, rows), rows)

    def target(t):
        half = lax.div(t + 1, 2)
        return lax.rem(me + n // 2 + (2 * lax.rem(t, 2) - 1) * half, n)

    barrier = pltpu.get_barrier_semaphore()

    @pl.loop(0, n - 1)
    def _(t):
        pl.semaphore_signal(
            barrier,
            inc=1,
            device_id={"node": target(t)},
            device_id_type=pl.DeviceIdType.MESH,
        )

    pl.semaphore_wait(barrier, n - 1)

    def push(src, dst, send_sem, recv_sem, to):
        pltpu.make_async_remote_copy(
            src_ref=src,
            dst_ref=dst,
            send_sem=send_sem,
            recv_sem=recv_sem,
            device_id={"node": to},
            device_id_type=pl.DeviceIdType.MESH,
        ).start()

    def landed(ref, sem):
        pltpu.make_async_copy(ref, ref, sem).wait()

    @pl.loop(0, n - 1)
    def _(t):
        to = target(t)
        push(left_send.at[to], lefts.at[lax.rem(to, 2), :, my_rows], left_out_sem, left_sem, to)

    pltpu.make_async_copy(left_send.at[me], lefts.at[parity, :, my_rows], left_sem).start()

    @pl.loop(0, n - 1)
    def _(t):
        to = target(t)
        push(a_send.at[to], a_full.at[:, my_rows], a_out_sem, a_sem, to)

    pltpu.make_async_copy(a_send.at[me], a_full.at[:, my_rows], a_sem).start()

    def push_right(c):
        @pl.loop(0, n - 1)
        def _(t):
            to = target(t)
            push(b_send.at[c, to], b_full.at[c, :, my_rows], b_out_sem.at[c], b_sem.at[c], to)

        pltpu.make_async_copy(b_send.at[c, me], b_full.at[c, :, my_rows], b_sem.at[c]).start()

    for c in range(min(AHEAD, chunks)):
        push_right(c)

    landed(lefts.at[parity], left_sem)
    push(lefts.at[parity], lefts.at[parity], swap_out_sem, swap_sem, partner)
    landed(lefts.at[1 - parity], swap_sem)

    def block(i):
        return pl.ds(pl.multiple_of(i * TILE, TILE), TILE)

    @pl.loop(0, tiles * tiles)
    def _(t):
        down, across = block(lax.div(t, tiles)), block(lax.rem(t, tiles))
        real_part, imag_part = tile_product(
            lefts[0, 0, down, :], lefts[0, 1, down, :], lefts[1, 0, :, across], lefts[1, 1, :, across]
        )
        left_plain[0, down, across] = real_part
        left_plain[1, down, across] = imag_part

    half = n // 2
    slots = merged.shape[1]
    near, far = pl.ds(0, half), pl.ds(half, slots)
    side, place = lax.div(me, half), lax.rem(me, half)
    mirror = lax.rem(me + half, n)

    def rows_of(device):
        return pl.ds(pl.multiple_of(device * rows, rows), rows)

    for c in range(chunks):
        panels[c][half + slots] = jnp.zeros(panels[c].shape[1:], panels[c].dtype)
        relayed[c][half] = jnp.zeros(relayed[c].shape[1:], relayed[c].dtype)

    flipped = flags[me] == 1

    @pl.loop(0, tiles * tiles)
    def _(t):
        down, across = block(lax.div(t, tiles)), block(lax.rem(t, tiles))
        left_used[0, down, across] = jnp.where(
            flipped, left_plain[0, across, down].T, left_plain[0, down, across]
        )
        left_used[1, down, across] = jnp.where(
            flipped, -left_plain[1, across, down].T, left_plain[1, down, across]
        )

    landed(a_full, a_sem)

    def compute(c):
        landed(b_full.at[c], b_sem.at[c])

        @pl.loop(0, tiles)
        def _(i):
            down = block(i)
            real_part, imag_part = tile_product(
                a_full[0, down, :], a_full[1, down, :], b_full[c, 0], b_full[c, 1]
            )
            right_pair[0, down, :] = real_part
            right_pair[1, down, :] = imag_part

        @pl.loop(0, tiles)
        def _(i):
            down = block(i)
            real_part, imag_part = tile_product(
                left_used[0, down, :], left_used[1, down, :], right_pair[0], right_pair[1]
            )
            result[c, 0, down, :] = real_part
            result[c, 1, down, :] = imag_part

        @pl.loop(1, half)
        def _(t):
            to = side * half + lax.rem(place + t, half)
            push(
                result.at[c, :, rows_of(lax.rem(to + half, n))],
                relayed[c].at[place],
                relay_out_sem.at[c],
                relay_sem.at[c],
                to,
            )

        pltpu.make_async_copy(
            result.at[c, :, rows_of(mirror)], relayed[c].at[place], relay_sem.at[c]
        ).start()

        @pl.loop(1, half)
        def _(t):
            to = side * half + lax.rem(place + t, half)
            push(
                result.at[c, :, rows_of(to)],
                panels[c].at[place],
                result_out_sem.at[c],
                result_sem.at[c],
                to,
            )

        pltpu.make_async_copy(
            result.at[c, :, my_rows], panels[c].at[place], result_sem.at[c]
        ).start()

    def merge(c):
        landed(relayed[c].at[near], relay_sem.at[c])

        @pl.loop(0, slots)
        def _(t):
            at = 2 * (side * slots + t)
            first = relayed[c][merges[at]].astype(jnp.float32)
            second = relayed[c][merges[at + 1]].astype(jnp.float32)
            merged[c, t] = (first + second).astype(merged.dtype)

        push(merged.at[c], panels[c].at[far], far_out_sem.at[c], far_sem.at[c], mirror)

    for c in range(chunks):
        compute(c)
        if c + AHEAD < chunks:
            push_right(c + AHEAD)
        if c > 0:
            merge(c - 1)
    merge(chunks - 1)

    width = b_full.shape[-1]
    for c in range(chunks):
        landed(panels[c].at[near], result_sem.at[c])
        landed(panels[c].at[far], far_sem.at[c])

        @pl.loop(0, out.shape[0])
        def _(d):
            at = 2 * (side * out.shape[0] + d)
            first = panels[c][finals[at]].astype(jnp.float32)
            second = panels[c][finals[at + 1]].astype(jnp.float32)
            out[d, :, :, c * width : (c + 1) * width] = (first + second).astype(out.dtype)

    others = pl.ds(0, n - 1)
    others_near = pl.ds(0, half - 1)
    landed(left_send.at[others], left_out_sem)
    landed(a_send.at[others], a_out_sem)
    landed(lefts.at[parity], swap_out_sem)
    for c in range(chunks):
        landed(b_send.at[c, others], b_out_sem.at[c])
        landed(panels[c].at[others_near], result_out_sem.at[c])
        landed(relayed[c].at[others_near], relay_out_sem.at[c])
        landed(merged.at[c], far_out_sem.at[c])


def local(nodes, pair_nodes, prod_left, prod_right, prod_flag, prod_diag, *, n):
    _, parts, rows, order = nodes.shape
    count = prod_left.shape[0]
    assert count == n == pair_nodes.shape[0] and rows * n == order
    half = diags = count // 2
    slots = half // 2 + 1
    chunks = order // WIDTH
    flags, merges, finals, left_send, a_send, b_send = plan_and_gather(
        nodes, pair_nodes, prod_left, prod_right, prod_flag, prod_diag, chunks
    )
    width = order // chunks
    kind = nodes.dtype
    dma = pltpu.SemaphoreType.DMA
    smem = pl.BlockSpec(memory_space=pltpu.SMEM)
    anywhere = pl.BlockSpec(memory_space=pl.ANY)
    return pl.pallas_call(
        functools.partial(exchange_kernel, n),
        out_shape=jax.ShapeDtypeStruct((diags, parts, rows, order), kind),
        in_specs=[smem, smem, smem, anywhere, anywhere, anywhere],
        out_specs=pl.BlockSpec(memory_space=pltpu.VMEM),
        scratch_shapes=[
            pltpu.VMEM((2, parts, order, order), kind),
            pltpu.VMEM((parts, order, order), kind),
            pltpu.VMEM((chunks, parts, order, width), kind),
            pltpu.VMEM((parts, order, order), kind),
            pltpu.VMEM((parts, order, order), kind),
            pltpu.VMEM((parts, order, width), kind),
            pltpu.VMEM((chunks, parts, order, width), kind),
            [pltpu.VMEM((half + slots + 1, parts, rows, width), kind)] * chunks,
            [pltpu.VMEM((half + 1, parts, rows, width), kind)] * chunks,
            pltpu.VMEM((chunks, slots, parts, rows, width), kind),
            dma,
            dma,
            dma((chunks,)),
            dma,
            dma((chunks,)),
            dma((chunks,)),
            dma((chunks,)),
            dma,
            dma,
            dma((chunks,)),
            dma,
            dma((chunks,)),
            dma((chunks,)),
            dma((chunks,)),
        ],
        compiler_params=pltpu.CompilerParams(
            collective_id=0, has_side_effects=True, vmem_limit_bytes=38 * 2**20
        ),
    )(flags, merges, finals, left_send, a_send, b_send)


def solution(mesh):
    placed = (P("grp", None, "node", None), P(), P(), P(), P(), P())
    return jax.shard_map(
        functools.partial(local, n=mesh.shape["node"]),
        mesh=mesh,
        in_specs=placed,
        out_specs=P("grp", None, "node", None),
        check_vma=False,
    )
```
